32 devices in a mesh: row: 8 (over z, y), col: 4 (over x, core).
Axes of the slice: x: 2, y: 2, z: 4, core: 2. Of those that a mesh axis runs over, the one named last changes fastest.
Arguments:
- tensor: bfloat16 [2048, 8192], P(('row', 'col')), may hold values from -6 to 6
- density: bfloat16 [2, 4096, 8192], P(None, 'col', 'row'), may hold values from -0.125 to 0.125
- tensor_mask: int32 [16, 64], replicated, may hold values 0 or 1
- density_mask: int32 [64, 64], replicated, may hold values 0 or 1
- pair_rows: int32 [32], replicated, may hold values from 0 to 31, as said below
Outputs:
- contracted: bfloat16 [2048, 8192], P(('row', 'col'))
The draws below stay inside these ranges and needn't reach their ends.
Inputs may be any that keep to these rules, and one draw needn't show every extreme that they name: pair_rows is a permutation of 0 to 31. Among the 8 slots that share one remainder modulo 4, at most 3 hold units of any one group of 8 consecutive units, and for every remainder some group gets exactly 3.
All inputs are finite; a program needn't handle non-finite values.
Results may differ from the reference program's by a relative error of at most 0.001.
Values may be sent and summed in bfloat16 or wider, within the bound.
A program may use at most 64 MiB of HBM per device.

```python
import jax
import jax.numpy as jnp
from jax import lax

N = 8192
UNIT = 64
BLOCK = 128
ROWS = 2048
RB = 16
NB = 64
N_ROW = 8
N_COL = 4


def draw_pair_rows(key, part):
    key_perm, key_shift, key_rows, key_order = jax.random.split(key, 4)
    column_perm = jax.random.permutation(key_perm, N_COL).astype(jnp.int32)
    offset = jax.random.randint(key_shift, (), 1, N_COL, dtype=jnp.int32)
    positions = jnp.arange(N_ROW, dtype=jnp.int32)
    groups = jnp.broadcast_to(positions // 2, (N_COL, N_ROW))
    dropped = 2 * ((column_perm + offset) % N_COL)
    groups = jnp.where(positions[None, :] == dropped[:, None], column_perm[:, None], groups)
    row_seeds = jax.random.split(key_rows, N_COL)
    groups = jax.vmap(jax.random.permutation)(row_seeds, groups)
    flat_groups = groups.T.reshape(-1)
    visit_order = jax.random.permutation(key_order, N_ROW * N_COL)
    ordered = flat_groups[visit_order]
    onehot = (ordered[:, None] == jnp.arange(N_COL, dtype=jnp.int32)[None, :]).astype(jnp.int32)
    earlier = jnp.cumsum(onehot, axis=0) - onehot
    within = jnp.sum(earlier * onehot, axis=1)
    return jnp.zeros((N_ROW * N_COL,), jnp.int32).at[visit_order].set(ordered * N_ROW + within)


def touch_ends(drawn, key, smallest, largest):
    spot = [jax.random.randint(jax.random.fold_in(key, axis), (), 0, length) for axis, length in enumerate(drawn.shape)]
    main_axis = drawn.shape.index(max(drawn.shape))
    next_to = spot[:main_axis] + [(spot[main_axis] + 1) % drawn.shape[main_axis]] + spot[main_axis + 1:]
    return drawn.at[tuple(spot)].set(smallest).at[tuple(next_to)].set(largest)


def block_levels(own_key, dims, cuts, low, top_value):
    factor_of, own = 1.0, jax.random.fold_in(own_key, 6)
    for dim, shards_of in cuts:
        heights = jnp.exp(jax.random.uniform(jax.random.fold_in(own, dim), (shards_of,), jnp.float32, low / len(cuts), top_value / len(cuts)))
        factor_of = factor_of * jnp.repeat(heights, dims[dim] // shards_of).reshape([-1 if axis == dim else 1 for axis in range(len(dims))])
    return factor_of


def scatter_about(rng, extent, width, most, pieces=(), kind=jnp.bfloat16):
    result = jax.random.normal(rng, extent, jnp.float32) * width
    if len(pieces) > 0:
        result = block_levels(rng, extent, pieces, -0.22, 0.18) * result
    return jnp.clip(result, min=-most, max=most).astype(kind)


def setup_inputs(seed: int = 0) -> dict:
    key_of = jax.random.split(jax.random.key(seed), 6)
    tensor = scatter_about(key_of[0], (ROWS, N), 1.0, 6.0, ((0, 32),))
    density = scatter_about(key_of[1], (2, N // 2, N), (N // 4) ** -0.5, 0.125, ((1, 4), (2, 8)))
    tensor_mask = touch_ends((jax.random.randint(key_of[2], (RB, NB), 0, 2) < 1).astype(jnp.int32), jax.random.fold_in(key_of[2], 1), 0, 1)
    density_mask = touch_ends((jax.random.randint(key_of[3], (NB, NB), 0, 2) < 1).astype(jnp.int32), jax.random.fold_in(key_of[3], 1), 0, 1)
    pair_rows = draw_pair_rows(jax.random.fold_in(key_of[5], 71), 0)
    return dict(tensor=tensor, density=density, tensor_mask=tensor_mask, density_mask=density_mask, pair_rows=pair_rows)


def reference(tensor, density, tensor_mask, density_mask, pair_rows):
    row_index = (pair_rows[:, None] * UNIT + jnp.arange(UNIT, dtype=jnp.int32)[None, :]) // BLOCK
    row_mask = jnp.take(tensor_mask, row_index.reshape(-1), axis=0).astype(jnp.bfloat16)
    masked = tensor * jnp.repeat(row_mask, BLOCK, axis=1)
    full_mask = jnp.repeat(jnp.repeat(density_mask.astype(jnp.bfloat16), BLOCK, axis=0), BLOCK, axis=1)
    density_full = density.reshape(N, N) * full_mask
    product = jnp.dot(masked.astype(jnp.float32), density_full.astype(jnp.float32),
                      preferred_element_type=jnp.float32, precision=lax.Precision.HIGHEST)
    return product.astype(jnp.bfloat16)
```

```python
import functools

import jax
import jax.numpy as jnp
from jax import lax
from jax.experimental import pallas as pl
from jax.experimental.pallas import tpu as pltpu
from jax.sharding import PartitionSpec as P

BLOCK = 128
CORES = 2
MESH = pl.DeviceIdType.MESH


def kernel(
    dims, t_ref, d_ref, tm_ref, dm_ref, pr_ref, out_ref,
    a_raw, a_m, b_raw, b_m, acc, res,
    a_recv, a_send, b_recv, b_send, o_recv, o_send, loc,
):
    n_row, n_col, hi_n, lo_n, x_n, chunks = dims
    r = lax.axis_index("row")
    c = lax.axis_index("col")
    hi, lo = r // lo_n, r % lo_n
    x, core = c // CORES, c % CORES
    rows, orbitals = t_ref.shape
    piece_rows, width = d_ref.shape[1], d_ref.shape[2]
    half = orbitals // 2
    w = width // chunks
    late = []

    def when_static(cond, body):
        if cond is True:
            body()
        else:
            pl.when(cond)(body)

    barrier = pltpu.get_barrier_semaphore()

    def greet(peer):
        pl.semaphore_signal(barrier, inc=1, device_id=peer, device_id_type=MESH)

    for q in range(1, n_row):
        greet(((r + q) % n_row, c))
    greet((r, x * CORES + (core + 1) % CORES))
    pl.when(x > 0)(lambda: greet((r, c - CORES)))
    pl.when(x < x_n - 1)(lambda: greet((r, c + CORES)))
    expected = n_row + (x > 0).astype(jnp.int32) + (x < x_n - 1).astype(jnp.int32)
    pl.semaphore_wait(barrier, expected)

    def row_of(h, l):
        return h * lo_n + l

    def slot_of(h, l):
        return l * hi_n + h

    def a_copy(way, h, l, dest, own=False):
        s = slot_of(h, l)
        return pltpu.make_async_remote_copy(
            src_ref=t_ref if own else a_raw.at[s],
            dst_ref=a_raw.at[s],
            send_sem=a_send.at[way, s],
            recv_sem=a_recv.at[s],
            device_id=(dest, c),
            device_id_type=MESH,
        )

    def a_go(cond, way, h, l, dest, own=False):
        when_static(cond, lambda: a_copy(way, h, l, dest, own).start())
        late.append((cond, lambda: a_copy(way, h, l, dest, own).wait_send()))

    def a_wait(h, l):
        a_copy(0, h, l, r).wait_recv()

    def a_lo_go(cond, h, own=False):
        left = lo > 0
        right = lo < lo_n - 1
        a_go(jnp.logical_and(cond, left), 2, h, lo, r - 1, own)
        a_go(jnp.logical_and(cond, right), 3, h, lo, r + 1, own)

    def b_copy(way, j, cc, dest, own=False):
        return pltpu.make_async_remote_copy(
            src_ref=d_ref.at[:, :, pl.ds(j * w, w)] if own else b_raw.at[cc, j],
            dst_ref=b_raw.at[cc, j],
            send_sem=b_send.at[way, cc, j],
            recv_sem=b_recv.at[cc, j],
            device_id=(r, dest),
            device_id_type=MESH,
        )

    def b_go(cond, way, j, cc, dest, own=False):
        when_static(cond, lambda: b_copy(way, j, cc, dest, own).start())
        late.append((cond, lambda: b_copy(way, j, cc, dest, own).wait_send()))

    def b_wait(j, cc):
        b_copy(0, j, cc, c).wait_recv()

    other = x * CORES + (core + 1) % CORES
    own_slot = slot_of(hi, lo)
    true = hi >= 0

    a_go(hi > 0, 0, hi, lo, row_of(hi - 1, lo), own=True)
    a_go(hi < hi_n - 1, 1, hi, lo, row_of(hi + 1, lo), own=True)
    a_lo_go(true, hi, own=True)
    for j in range(chunks):
        b_go(x > 0, 0, j, c, c - CORES, own=True)
        b_go(x < x_n - 1, 1, j, c, c + CORES, own=True)
    own_a = pltpu.make_async_copy(t_ref, a_raw.at[own_slot], loc.at[chunks])
    own_a.start()
    own_b = [
        pltpu.make_async_copy(d_ref.at[:, :, pl.ds(j * w, w)], b_raw.at[c, j], loc.at[j])
        for j in range(chunks)
    ]
    for j in range(chunks):
        own_b[j].start()
        b_go(True, 2, j, c, other, own=True)

    def mask_a(h, l):
        s = slot_of(h, l)
        unit = pr_ref[row_of(h, l) * n_col + c]
        mask_row = (unit * rows) // BLOCK

        def body(jb, _):
            m = tm_ref[mask_row, jb].astype(jnp.float32)
            mv = jnp.full((16, BLOCK), m, jnp.float32).astype(jnp.bfloat16)
            cols = pl.ds(pl.multiple_of(jb * BLOCK, BLOCK), BLOCK)
            v = a_raw[s, :, cols].reshape(rows // 16, 16, BLOCK) * mv[None]
            a_m[l, pl.ds(pl.multiple_of(h * rows, rows), rows), cols] = v.reshape(rows, BLOCK)
            return 0

        lax.fori_loop(0, orbitals // BLOCK, body, 0)

    blocks_k = piece_rows // BLOCK

    def mask_b(j):
        def body(i, _):
            kb = i % blocks_k
            ch = i // blocks_k
            cc, h = ch // 2, ch % 2
            src = pl.ds(pl.multiple_of(kb * BLOCK, BLOCK), BLOCK)
            k = h * half + cc * piece_rows + kb * BLOCK
            dst = pl.ds(pl.multiple_of(k, BLOCK), BLOCK)
            for jb in range(w // BLOCK):
                m = dm_ref[k // BLOCK, (r * width + j * w) // BLOCK + jb].astype(jnp.float32)
                mv = jnp.full((16, BLOCK), m, jnp.float32).astype(jnp.bfloat16)
                cols = pl.ds(jb * BLOCK, BLOCK)
                v = b_raw[cc, j, h, src, cols].reshape(BLOCK // 16, 16, BLOCK) * mv[None]
                b_m[j, dst, cols] = v.reshape(BLOCK, BLOCK)
            return 0

        lax.fori_loop(0, n_col * 2 * blocks_k, body, 0)

    kc = orbitals // 4

    def o_copy(q, h, j, dest, sender):
        return pltpu.make_async_remote_copy(
            src_ref=res.at[q, j, pl.ds(h * rows, rows)],
            dst_ref=out_ref.at[:, pl.ds(pl.multiple_of(sender * width + j * w, BLOCK), w)],
            send_sem=o_send.at[q, h, j],
            recv_sem=o_recv.at[sender, j],
            device_id=(dest, c),
            device_id_type=MESH,
        )

    def o_local(h, j):
        return pltpu.make_async_copy(
            res.at[0, j, pl.ds(h * rows, rows)],
            out_ref.at[:, pl.ds(pl.multiple_of(r * width + j * w, BLOCK), w)],
            o_send.at[0, h, j],
        )

    def unit(q, j):
        g = (lo + q) % lo_n
        acc[...] = jnp.zeros_like(acc)

        def body(k, _):
            ks = pl.ds(pl.multiple_of(k * kc, kc), kc)
            acc[...] += jnp.dot(a_m[g, :, ks], b_m[j, ks, :], preferred_element_type=jnp.float32)
            return 0

        lax.fori_loop(0, orbitals // kc, body, 0)
        res[q, j] = acc[...].astype(jnp.bfloat16)
        for h in range(hi_n):
            dest = row_of(h, g)
            if q == 0:
                pl.when(hi != h)(lambda: o_copy(q, h, j, dest, r).start())
                pl.when(hi == h)(lambda: o_local(h, j).start())
                late.append((hi != h, functools.partial(
                    lambda q, h, j, dest: o_copy(q, h, j, dest, r).wait_send(), q, h, j, dest)))
                late.append((hi == h, functools.partial(lambda h, j: o_local(h, j).wait(), h, j)))
            else:
                o_copy(q, h, j, dest, r).start()
                late.append((True, functools.partial(
                    lambda q, h, j, dest: o_copy(q, h, j, dest, r).wait_send(), q, h, j, dest)))

    def b_arrive(j):
        for e in range(1, x_n):
            for sign in (-1, 1):
                xx = x + sign * e
                there = jnp.logical_and(xx >= 0, xx < x_n)
                cc = xx * CORES + core
                pl.when(there)(lambda: b_wait(j, cc))
                onward = x - sign
                more = jnp.logical_and(there, jnp.logical_and(onward >= 0, onward < x_n))
                b_go(more, 0 if sign > 0 else 1, j, cc, onward * CORES + core)
                b_go(there, 2, j, cc, other)

    def b_finish(j):
        own_b[j].wait()
        for xx in range(x_n):
            b_wait(j, xx * CORES + (core + 1) % CORES)
        mask_b(j)

    def line_arrive(d):
        for sign in (-1, 1):
            h = hi + sign * d
            there = jnp.logical_and(h >= 0, h < hi_n)
            pl.when(there)(lambda: a_wait(h, lo))
            onward = hi - sign
            more = jnp.logical_and(there, jnp.logical_and(onward >= 0, onward < hi_n))
            a_go(more, 0 if sign > 0 else 1, h, lo, row_of(onward, lo))
            a_lo_go(there, h)

    def at_distance(d):
        if d == 0:
            return [(hi, true)]
        out = []
        for sign in (-1, 1):
            h = hi + sign * d
            out.append((h, jnp.logical_and(h >= 0, h < hi_n)))
        return out

    def lo_arrive(d):
        for h, there in at_distance(d):
            for e in range(1, lo_n):
                for sign in (-1, 1):
                    l = lo + sign * e
                    ok = jnp.logical_and(there, jnp.logical_and(l >= 0, l < lo_n))
                    pl.when(ok)(lambda: a_wait(h, l))
                    onward = lo - sign
                    more = jnp.logical_and(ok, jnp.logical_and(onward >= 0, onward < lo_n))
                    a_go(more, 2 if sign > 0 else 3, h, l, row_of(hi, onward))

    def mask_lo(d):
        for h, there in at_distance(d):
            for q in range(1, lo_n):
                g = (lo + q) % lo_n
                pl.when(there)(lambda: mask_a(h, g))

    def mask_line(d):
        for h, there in at_distance(d):
            pl.when(there)(lambda: mask_a(h, lo))

    own_a.wait()
    mask_line(0)
    for d in range(1, hi_n):
        line_arrive(d)
        b_arrive(d - 1)
        lo_arrive(d - 1)
        mask_line(d)
        mask_lo(d - 1)
        b_finish(d - 1)
    for j in range(hi_n - 1):
        unit(0, j)
    for j in range(hi_n - 1, chunks):
        b_arrive(j)
    lo_arrive(hi_n - 1)
    mask_lo(hi_n - 1)
    for j in range(hi_n - 1):
        for q in range(1, lo_n):
            unit(q, j)
    for j in range(hi_n - 1, chunks):
        b_finish(j)
        for q in range(lo_n):
            unit(q, j)

    for q in range(1, n_row):
        sender = (r + q) % n_row
        for j in range(chunks):
            o_copy(0, 0, j, r, sender).wait_recv()
    for cond, wait in late:
        when_static(cond, wait)


def on_device(dims, tensor, density, tensor_mask, density_mask, pair_rows):
    n_row, n_col, hi_n, lo_n, x_n, chunks = dims
    rows, orbitals = tensor.shape
    _, piece_rows, width = density.shape
    w = width // chunks
    bf16 = jnp.bfloat16
    any_spec = pl.BlockSpec(memory_space=pl.ANY)
    smem = pl.BlockSpec(memory_space=pltpu.SMEM)
    return pl.pallas_call(
        functools.partial(kernel, dims),
        out_shape=jax.ShapeDtypeStruct((rows, orbitals), bf16),
        in_specs=[any_spec, any_spec, smem, smem, smem],
        out_specs=any_spec,
        scratch_shapes=[
            pltpu.VMEM((n_row, rows, orbitals), bf16),
            pltpu.VMEM((lo_n, hi_n * rows, orbitals), bf16),
            pltpu.VMEM((n_col, chunks, 2, piece_rows, w), bf16),
            pltpu.VMEM((chunks, orbitals, w), bf16),
            pltpu.VMEM((hi_n * rows, w), jnp.float32),
            pltpu.VMEM((lo_n, chunks, hi_n * rows, w), bf16),
            pltpu.SemaphoreType.DMA((n_row,)),
            pltpu.SemaphoreType.DMA((4, n_row)),
            pltpu.SemaphoreType.DMA((n_col, chunks)),
            pltpu.SemaphoreType.DMA((3, n_col, chunks)),
            pltpu.SemaphoreType.DMA((n_row, chunks)),
            pltpu.SemaphoreType.DMA((lo_n, hi_n, chunks)),
            pltpu.SemaphoreType.DMA((chunks + 1,)),
        ],
        compiler_params=pltpu.CompilerParams(
            collective_id=0, has_side_effects=True, vmem_limit_bytes=60 << 20
        ),
    )(tensor, density, tensor_mask, density_mask, pair_rows)


def solution(mesh):
    n_row, n_col = mesh.shape["row"], mesh.shape["col"]
    hi_n = 1
    while hi_n * hi_n < n_row:
        hi_n *= 2
    dims = (n_row, n_col, hi_n, n_row // hi_n, n_col // CORES, max(4, hi_n))
    placed = (P(("row", "col"), None), P(None, "col", "row"), P(), P(), P())
    return jax.shard_map(
        functools.partial(on_device, dims),
        mesh=mesh,
        in_specs=placed,
        out_specs=P(("row", "col"), None),
        check_vma=False,
    )
```

```python
import functools
import math

import jax
import jax.numpy as jnp
from jax import lax
from jax.experimental import pallas as pl
from jax.experimental.pallas import tpu as pltpu
from jax.sharding import PartitionSpec as P

BLOCK = 128
CORES = 2
MESH = pl.DeviceIdType.MESH


def kernel(
    dims, room, pa_ref, pb_ref, tm_ref, dm_ref, pr_ref, out_ref,
    a_raw, a_m, b_raw, b_m, acc, res,
    a_recv, a_send, b_recv, b_send, o_recv, o_send, loc, *stage,
):
    n_row, n_col, hi_n, lo_n, x_n, chunks = dims
    a_room, b_room = room
    piece = b_room // chunks
    a_stage, b_stage, staged = stage if stage else (None, None, None)
    r = lax.axis_index("row")
    c = lax.axis_index("col")
    hi, lo = r // lo_n, r % lo_n
    x, core = c // CORES, c % CORES
    rows = pa_ref.shape[1]
    orbitals = out_ref.shape[1]
    piece_rows, width = orbitals // 2 // n_col, orbitals // n_row
    half = orbitals // 2
    w = width // chunks
    late = []

    def when_static(cond, body):
        if cond is True:
            body()
        else:
            pl.when(cond)(body)

    barrier = pltpu.get_barrier_semaphore()

    def greet(peer):
        pl.semaphore_signal(barrier, inc=1, device_id=peer, device_id_type=MESH)

    for q in range(1, n_row):
        greet(((r + q) % n_row, c))
    greet((r, x * CORES + (core + 1) % CORES))
    pl.when(x > 0)(lambda: greet((r, c - CORES)))
    pl.when(x < x_n - 1)(lambda: greet((r, c + CORES)))
    expected = n_row + (x > 0).astype(jnp.int32) + (x < x_n - 1).astype(jnp.int32)
    pl.semaphore_wait(barrier, expected)

    def row_of(h, l):
        return h * lo_n + l

    def slot_of(h, l):
        return l * hi_n + h

    def a_copy(way, h, l, dest, own=False):
        s = slot_of(h, l)
        return pltpu.make_async_remote_copy(
            src_ref=pa_ref if own else a_raw.at[s],
            dst_ref=a_raw.at[s],
            send_sem=a_send.at[way, s],
            recv_sem=a_recv.at[s],
            device_id=(dest, c),
            device_id_type=MESH,
        )

    def a_go(cond, way, h, l, dest, own=False):
        when_static(cond, lambda: a_copy(way, h, l, dest, own).start())
        late.append((cond, lambda: a_copy(way, h, l, dest, own).wait_send()))

    def a_wait(h, l):
        a_copy(0, h, l, r).wait_recv()

    def a_lo_go(cond, h, own=False):
        left = lo > 0
        right = lo < lo_n - 1
        a_go(jnp.logical_and(cond, left), 2, h, lo, r - 1, own)
        a_go(jnp.logical_and(cond, right), 3, h, lo, r + 1, own)

    def b_part(p):
        return pl.ds(p * piece, piece)

    def b_copy(way, p, cc, dest, own=False):
        return pltpu.make_async_remote_copy(
            src_ref=pb_ref.at[b_part(p)] if own else b_raw.at[cc, b_part(p)],
            dst_ref=b_raw.at[cc, b_part(p)],
            send_sem=b_send.at[way, cc, p],
            recv_sem=b_recv.at[cc, p],
            device_id=(r, dest),
            device_id_type=MESH,
        )

    def b_go(cond, way, j, cc, dest, own=False):
        when_static(cond, lambda: b_copy(way, j, cc, dest, own).start())
        late.append((cond, lambda: b_copy(way, j, cc, dest, own).wait_send()))

    def b_wait(j, cc):
        b_copy(0, j, cc, c).wait_recv()

    other = x * CORES + (core + 1) % CORES
    own_slot = slot_of(hi, lo)
    true = hi >= 0

    a_go(hi > 0, 0, hi, lo, row_of(hi - 1, lo), own=True)
    a_go(hi < hi_n - 1, 1, hi, lo, row_of(hi + 1, lo), own=True)
    a_lo_go(true, hi, own=True)
    for j in range(chunks):
        b_go(x > 0, 0, j, c, c - CORES, own=True)
        b_go(x < x_n - 1, 1, j, c, c + CORES, own=True)
    own_a = pltpu.make_async_copy(pa_ref, a_raw.at[own_slot], loc.at[chunks])
    own_a.start()
    own_b = [
        pltpu.make_async_copy(
            pb_ref.at[b_part(j)], (b_stage if stage else b_raw).at[c, b_part(j)], loc.at[j])
        for j in range(chunks)
    ]
    for j in range(chunks):
        own_b[j].start()
        b_go(True, 2, j, c, other, own=True)

    def mask_vector(m):
        return jnp.full((16, BLOCK), m.astype(jnp.float32), jnp.float32).astype(jnp.bfloat16)

    def mask_a(h, l):
        s = slot_of(h, l)
        unit = pr_ref[row_of(h, l) * n_col + c]
        mask_row = (unit * rows) // BLOCK

        if stage:
            move = pltpu.make_async_copy(a_raw.at[s], a_stage, staged.at[n_col])
            move.start()
            move.wait()

        def body(jb, count):
            m = tm_ref[mask_row, jb]
            if stage:
                v = a_stage[jnp.minimum(count, a_room - 1)]
            else:
                v = a_raw[s, jb]
            v = v.reshape(rows // 16, 16, BLOCK)
            cols = pl.ds(pl.multiple_of(jb * BLOCK, BLOCK), BLOCK)
            to = pl.ds(pl.multiple_of(h * rows, rows), rows)
            a_m[l, to, cols] = (v * mask_vector(m)[None]).reshape(rows, BLOCK)
            return count + m

        lax.fori_loop(0, orbitals // BLOCK, body, jnp.int32(0))

    blocks_k = piece_rows // BLOCK
    seen = [jnp.int32(0)] * n_col

    def mask_b(j):
        for cc in range(n_col):
            def body(i, count):
                h, kb = i // blocks_k, i % blocks_k
                k = h * half + cc * piece_rows + kb * BLOCK
                to = pl.ds(pl.multiple_of(k, BLOCK), BLOCK)
                for jb in range(w // BLOCK):
                    m = dm_ref[k // BLOCK, (r * width + j * w) // BLOCK + jb]
                    if stage:
                        v = b_stage[cc, jnp.minimum(count, b_room - 1)]
                    else:
                        v = b_raw[cc, (j * 2 * blocks_k + i) * (w // BLOCK) + jb]
                    v = v.reshape(BLOCK // 16, 16, BLOCK)
                    cols = pl.ds(jb * BLOCK, BLOCK)
                    b_m[j, to, cols] = (v * mask_vector(m)[None]).reshape(BLOCK, BLOCK)
                    count = count + m
                return count

            seen[cc] = lax.fori_loop(0, 2 * blocks_k, body, seen[cc])

    kc = orbitals // 4

    far = jnp.where(hi < hi_n // 2, hi_n - 1, 0)
    near = jnp.where(hi < hi_n // 2, 0, 1)

    def o_copy(q, h, j, dest, sender):
        return pltpu.make_async_remote_copy(
            src_ref=res.at[q, j, pl.ds(pl.multiple_of(h * rows, rows), rows)],
            dst_ref=out_ref.at[:, pl.ds(pl.multiple_of(sender * width + j * w, BLOCK), w)],
            send_sem=o_send.at[q, h, j],
            recv_sem=o_recv.at[sender, j],
            device_id=(dest, c),
            device_id_type=MESH,
        )

    def o_local(h, j):
        return pltpu.make_async_copy(
            res.at[0, j, pl.ds(pl.multiple_of(h * rows, rows), rows)],
            out_ref.at[:, pl.ds(pl.multiple_of(r * width + j * w, BLOCK), w)],
            o_send.at[0, h, j],
        )

    def unit(q, j, start, count):
        g = (lo + q) % lo_n
        at = pl.ds(pl.multiple_of(start * rows, rows), count * rows)
        part = pl.ds(0, count * rows)
        acc[part] = jnp.zeros((count * rows, w), jnp.float32)

        def body(k, _):
            ks = pl.ds(pl.multiple_of(k * kc, kc), kc)
            acc[part] += jnp.dot(
                a_m[g, at, ks], b_m[j, ks, :], preferred_element_type=jnp.float32
            )
            return 0

        lax.fori_loop(0, orbitals // kc, body, 0)
        res[q, j, at] = acc[part].astype(jnp.bfloat16)
        for i in range(count):
            h = start + i
            dest = row_of(h, g)

            def wait_send(h=h, dest=dest):
                o_copy(q, h, j, dest, r).wait_send()

            def wait_local(h=h):
                o_local(h, j).wait()

            if q == 0:
                pl.when(hi != h)(lambda: o_copy(q, h, j, dest, r).start())
                pl.when(hi == h)(lambda: o_local(h, j).start())
                late.append((hi != h, wait_send))
                late.append((hi == h, wait_local))
            else:
                o_copy(q, h, j, dest, r).start()
                late.append((True, wait_send))

    def b_arrive(j):
        for e in range(1, x_n):
            for sign in (-1, 1):
                xx = x + sign * e
                there = jnp.logical_and(xx >= 0, xx < x_n)
                cc = xx * CORES + core
                pl.when(there)(lambda: b_wait(j, cc))
                onward = x - sign
                more = jnp.logical_and(there, jnp.logical_and(onward >= 0, onward < x_n))
                b_go(more, 0 if sign > 0 else 1, j, cc, onward * CORES + core)
                b_go(there, 2, j, cc, other)

    per_chunk = 2 * blocks_k * (w // BLOCK)
    needs = [-(-min(b_room, (j + 1) * per_chunk) // piece) for j in range(chunks)]

    def b_move(p, q):
        cc = (c + q) % n_col
        return pltpu.make_async_copy(
            b_raw.at[cc, b_part(p)], b_stage.at[cc, b_part(p)], staged.at[q])

    def b_finish(p):
        for xx in range(x_n):
            b_wait(p, xx * CORES + (core + 1) % CORES)
        if stage:
            for q in range(1, n_col):
                b_move(p, q).start()
            for q in range(1, n_col):
                b_move(p, q).wait()
            if p == 0:
                for own in own_b:
                    own.wait()
        else:
            own_b[p].wait()
        for j in range(chunks):
            if needs[j] == p + 1:
                mask_b(j)

    def line_arrive(d):
        for sign in (-1, 1):
            h = hi + sign * d
            there = jnp.logical_and(h >= 0, h < hi_n)
            pl.when(there)(lambda: a_wait(h, lo))
            onward = hi - sign
            more = jnp.logical_and(there, jnp.logical_and(onward >= 0, onward < hi_n))
            a_go(more, 0 if sign > 0 else 1, h, lo, row_of(onward, lo))
            a_lo_go(there, h)

    def at_distance(d):
        if d == 0:
            return [(hi, true)]
        out = []
        for sign in (-1, 1):
            h = hi + sign * d
            inside = jnp.logical_and(h >= 0, h < hi_n)
            out.append((h, jnp.logical_and(inside, h != far)))
        return out

    def lo_arrive(found):
        for h, there in found:
            for e in range(1, lo_n):
                for sign in (-1, 1):
                    l = lo + sign * e
                    ok = jnp.logical_and(there, jnp.logical_and(l >= 0, l < lo_n))
                    pl.when(ok)(lambda: a_wait(h, l))
                    onward = lo - sign
                    more = jnp.logical_and(ok, jnp.logical_and(onward >= 0, onward < lo_n))
                    a_go(more, 2 if sign > 0 else 3, h, l, row_of(hi, onward))
        for h, there in found:
            for q in range(1, lo_n):
                g = (lo + q) % lo_n
                pl.when(there)(lambda: mask_a(h, g))

    own_a.wait()
    mask_a(hi, lo)
    for d in range(1, hi_n):
        line_arrive(d)
        b_arrive(d - 1)
        for h, there in at_distance(d):
            pl.when(there)(lambda: mask_a(h, lo))
        lo_arrive(at_distance(d - 1))
        b_finish(d - 1)
    mask_a(far, lo)
    for p in range(hi_n - 1, chunks):
        b_arrive(p)
        b_finish(p)
    for j in range(chunks):
        unit(0, j, 0, hi_n)
    for j in range(chunks):
        for q in range(1, lo_n):
            unit(q, j, near, hi_n - 1)
    lo_arrive([(far, true)])
    for j in range(chunks):
        for q in range(1, lo_n):
            unit(q, j, far, 1)

    for q in range(1, n_row):
        sender = (r + q) % n_row
        for j in range(chunks):
            o_copy(0, 0, j, r, sender).wait_recv()
    for cond, wait in late:
        when_static(cond, wait)


def pack_kernel(dims, room, dense, t_ref, d_ref, tm_ref, dm_ref, pr_ref, pa_ref, pb_ref):
    n_row, n_col, _, _, _, chunks = dims
    a_room, b_room = room
    r = lax.axis_index("row")
    c = lax.axis_index("col")
    rows, orbitals = t_ref.shape
    _, piece_rows, width = d_ref.shape
    half, w = orbitals // 2, width // chunks
    blocks_k = piece_rows // BLOCK
    mask_row = (pr_ref[r * n_col + c] * rows) // BLOCK

    def a_body(jb, count):
        m = jnp.int32(1) if dense else tm_ref[mask_row, jb]

        @pl.when(jnp.logical_and(m > 0, count < a_room))
        def _():
            pa_ref[count] = t_ref[:, pl.ds(pl.multiple_of(jb * BLOCK, BLOCK), BLOCK)]

        return count + m

    a_count = lax.fori_loop(0, orbitals // BLOCK, a_body, jnp.int32(0))

    def a_clear(p, _):
        pa_ref[p] = jnp.zeros((rows, BLOCK), pa_ref.dtype)
        return 0

    lax.fori_loop(a_count, a_room, a_clear, 0)

    def b_body(i, count):
        kb, jh = i % blocks_k, i // blocks_k
        h, j = jh % 2, jh // 2
        k = h * half + c * piece_rows + kb * BLOCK
        for jb in range(w // BLOCK):
            m = jnp.int32(1) if dense else dm_ref[k // BLOCK, (r * width + j * w) // BLOCK + jb]

            @pl.when(jnp.logical_and(m > 0, count < b_room))
            def _():
                cols = pl.ds(pl.multiple_of(j * w + jb * BLOCK, BLOCK), BLOCK)
                pb_ref[count] = d_ref[h, pl.ds(pl.multiple_of(kb * BLOCK, BLOCK), BLOCK), cols]

            count = count + m
        return count

    b_count = lax.fori_loop(0, chunks * 2 * blocks_k, b_body, jnp.int32(0))

    def b_clear(p, _):
        pb_ref[p] = jnp.zeros((BLOCK, BLOCK), pb_ref.dtype)
        return 0

    lax.fori_loop(b_count, b_room, b_clear, 0)


def contract(dims, room, dense, number, tensor, density, tensor_mask, density_mask, pair_rows):
    n_row, n_col, hi_n, lo_n, x_n, chunks = dims
    a_room, b_room = room
    rows, orbitals = tensor.shape
    _, piece_rows, width = density.shape
    w = width // chunks
    bf16 = jnp.bfloat16
    any_spec = pl.BlockSpec(memory_space=pl.ANY)
    smem = pl.BlockSpec(memory_space=pltpu.SMEM)
    vmem = pl.BlockSpec(memory_space=pltpu.VMEM)
    packed = pl.pallas_call(
        functools.partial(pack_kernel, dims, room, dense),
        out_shape=[
            jax.ShapeDtypeStruct((a_room, rows, BLOCK), bf16),
            jax.ShapeDtypeStruct((b_room, BLOCK, BLOCK), bf16),
        ],
        in_specs=[vmem, vmem, smem, smem, smem],
        out_specs=[vmem, vmem],
        compiler_params=pltpu.CompilerParams(vmem_limit_bytes=60 << 20),
    )(tensor, density, tensor_mask, density_mask, pair_rows)
    return pl.pallas_call(
        functools.partial(kernel, dims, room),
        out_shape=jax.ShapeDtypeStruct((rows, orbitals), bf16),
        in_specs=[any_spec, any_spec, smem, smem, smem],
        out_specs=any_spec,
        scratch_shapes=[
            pltpu.VMEM((n_row, a_room, rows, BLOCK), bf16),
            pltpu.VMEM((lo_n, hi_n * rows, orbitals), bf16),
            pltpu.VMEM((n_col, b_room, BLOCK, BLOCK), bf16),
            pltpu.VMEM((chunks, orbitals, w), bf16),
            pltpu.VMEM((hi_n * rows, w), jnp.float32),
            pltpu.VMEM((lo_n, chunks, hi_n * rows, w), bf16),
            pltpu.SemaphoreType.DMA((n_row,)),
            pltpu.SemaphoreType.DMA((4, n_row)),
            pltpu.SemaphoreType.DMA((n_col, chunks)),
            pltpu.SemaphoreType.DMA((3, n_col, chunks)),
            pltpu.SemaphoreType.DMA((n_row, chunks)),
            pltpu.SemaphoreType.DMA((lo_n, hi_n, chunks)),
            pltpu.SemaphoreType.DMA((chunks + 1,)),
        ] + ([] if dense else [
            pltpu.VMEM((a_room, rows, BLOCK), bf16),
            pltpu.VMEM((n_col, b_room, BLOCK, BLOCK), bf16),
            pltpu.SemaphoreType.DMA((n_col + 1,)),
        ]),
        compiler_params=pltpu.CompilerParams(
            collective_id=number, has_side_effects=True, vmem_limit_bytes=60 << 20
        ),
    )(*packed, tensor_mask, density_mask, pair_rows)


def on_device(dims, *args):
    n_row, n_col, _, _, _, chunks = dims
    tensor, density, tensor_mask, density_mask, _ = args
    nb = tensor.shape[1] // BLOCK
    a_full = nb
    b_full = density.size // (BLOCK * BLOCK)

    def roomy(full, step):
        wanted = full // 2 + 2 * math.isqrt(full)
        return min(full, -(-wanted // step) * step)

    small = (roomy(a_full, 1), roomy(b_full, chunks))
    a_most = jnp.max(jnp.sum(tensor_mask, axis=1))
    b_most = jnp.max(jnp.sum(
        density_mask.reshape(2, n_col, nb // 2 // n_col, n_row, nb // n_row), axis=(0, 2, 4)))
    fits = jnp.logical_and(a_most <= small[0], b_most <= small[1])
    return lax.cond(
        fits,
        functools.partial(contract, dims, small, False, 0),
        functools.partial(contract, dims, (a_full, b_full), True, 1),
        *args,
    )


def solution(mesh):
    n_row, n_col = mesh.shape["row"], mesh.shape["col"]
    hi_n = 1
    while hi_n * hi_n < n_row:
        hi_n *= 2
    dims = (n_row, n_col, hi_n, n_row // hi_n, n_col // CORES, max(4, hi_n))
    placed = (P(("row", "col"), None), P(None, "col", "row"), P(), P(), P())
    return jax.shard_map(
        functools.partial(on_device, dims),
        mesh=mesh,
        in_specs=placed,
        out_specs=P(("row", "col"), None),
        check_vma=False,
    )
```

```python
import functools
import math

import jax
import jax.numpy as jnp
from jax import lax
from jax.experimental import pallas as pl
from jax.experimental.pallas import tpu as pltpu
from jax.sharding import PartitionSpec as P

BLOCK = 128
CORES = 2
MESH = pl.DeviceIdType.MESH


def kernel(
    dims, room, pa_ref, pb_ref, tm_ref, dm_ref, pr_ref, out_ref,
    a_raw, a_m, b_raw, b_m, acc, res,
    a_recv, a_send, b_recv, b_send, o_recv, o_send, loc, *stage,
):
    n_row, n_col, hi_n, lo_n, x_n, chunks = dims
    a_room, b_room = room
    piece = b_room // chunks
    a_stage, b_stage, staged = stage if stage else (None, None, None)
    r = lax.axis_index("row")
    c = lax.axis_index("col")
    hi, lo = r // lo_n, r % lo_n
    x, core = c // CORES, c % CORES
    rows = pa_ref.shape[1]
    orbitals = out_ref.shape[1]
    piece_rows, width = orbitals // 2 // n_col, orbitals // n_row
    half = orbitals // 2
    w = width // chunks
    late = []

    def when_static(cond, body):
        if cond is True:
            body()
        else:
            pl.when(cond)(body)

    barrier = pltpu.get_barrier_semaphore()

    def greet(peer):
        pl.semaphore_signal(barrier, inc=1, device_id=peer, device_id_type=MESH)

    for q in range(1, n_row):
        greet(((r + q) % n_row, c))
    greet((r, x * CORES + (core + 1) % CORES))
    pl.when(x > 0)(lambda: greet((r, c - CORES)))
    pl.when(x < x_n - 1)(lambda: greet((r, c + CORES)))
    expected = n_row + (x > 0).astype(jnp.int32) + (x < x_n - 1).astype(jnp.int32)
    pl.semaphore_wait(barrier, expected)

    def row_of(h, l):
        return h * lo_n + l

    def slot_of(h, l):
        return l * hi_n + h

    def a_copy(way, h, l, dest, own=False):
        s = slot_of(h, l)
        return pltpu.make_async_remote_copy(
            src_ref=pa_ref if own else a_raw.at[s],
            dst_ref=a_raw.at[s],
            send_sem=a_send.at[way, s],
            recv_sem=a_recv.at[s],
            device_id=(dest, c),
            device_id_type=MESH,
        )

    def a_go(cond, way, h, l, dest, own=False):
        when_static(cond, lambda: a_copy(way, h, l, dest, own).start())
        late.append((cond, lambda: a_copy(way, h, l, dest, own).wait_send()))

    def a_wait(h, l):
        a_copy(0, h, l, r).wait_recv()

    def a_lo_go(cond, h, own=False):
        left = lo > 0
        right = lo < lo_n - 1
        a_go(jnp.logical_and(cond, left), 2, h, lo, r - 1, own)
        a_go(jnp.logical_and(cond, right), 3, h, lo, r + 1, own)

    def b_part(p):
        return pl.ds(p * piece, piece)

    def b_copy(way, p, cc, dest, own=False):
        return pltpu.make_async_remote_copy(
            src_ref=pb_ref.at[b_part(p)] if own else b_raw.at[cc, b_part(p)],
            dst_ref=b_raw.at[cc, b_part(p)],
            send_sem=b_send.at[way, cc, p],
            recv_sem=b_recv.at[cc, p],
            device_id=(r, dest),
            device_id_type=MESH,
        )

    def b_go(cond, way, j, cc, dest, own=False):
        when_static(cond, lambda: b_copy(way, j, cc, dest, own).start())
        late.append((cond, lambda: b_copy(way, j, cc, dest, own).wait_send()))

    def b_wait(j, cc):
        b_copy(0, j, cc, c).wait_recv()

    other = x * CORES + (core + 1) % CORES
    own_slot = slot_of(hi, lo)
    true = hi >= 0

    a_go(hi > 0, 0, hi, lo, row_of(hi - 1, lo), own=True)
    a_go(hi < hi_n - 1, 1, hi, lo, row_of(hi + 1, lo), own=True)
    a_lo_go(true, hi, own=True)
    for j in range(chunks):
        b_go(x > 0, 0, j, c, c - CORES, own=True)
        b_go(x < x_n - 1, 1, j, c, c + CORES, own=True)
    own_a = pltpu.make_async_copy(pa_ref, a_raw.at[own_slot], loc.at[chunks])
    own_a.start()
    own_b = [
        pltpu.make_async_copy(
            pb_ref.at[b_part(j)], (b_stage if stage else b_raw).at[c, b_part(j)], loc.at[j])
        for j in range(chunks)
    ]
    for j in range(chunks):
        own_b[j].start()
        b_go(True, 2, j, c, other, own=True)

    def mask_vector(m):
        return jnp.full((16, BLOCK), m.astype(jnp.float32), jnp.float32).astype(jnp.bfloat16)

    def mask_a(h, l):
        s = slot_of(h, l)
        unit = pr_ref[row_of(h, l) * n_col + c]
        mask_row = (unit * rows) // BLOCK

        if stage:
            move = pltpu.make_async_copy(a_raw.at[s], a_stage, staged.at[n_col])
            move.start()
            move.wait()

        def body(jb, count):
            m = tm_ref[mask_row, jb]
            if stage:
                v = a_stage[jnp.minimum(count, a_room - 1)]
            else:
                v = a_raw[s, jb]
            v = v.reshape(rows // 16, 16, BLOCK)
            cols = pl.ds(pl.multiple_of(jb * BLOCK, BLOCK), BLOCK)
            to = pl.ds(pl.multiple_of(h * rows, rows), rows)
            a_m[l, to, cols] = (v * mask_vector(m)[None]).reshape(rows, BLOCK)
            return count + m

        lax.fori_loop(0, orbitals // BLOCK, body, jnp.int32(0))

    blocks_k = piece_rows // BLOCK
    seen = [jnp.int32(0)] * n_col

    def mask_b(j):
        for cc in range(n_col):
            def body(i, count):
                h, kb = i // blocks_k, i % blocks_k
                k = h * half + cc * piece_rows + kb * BLOCK
                to = pl.ds(pl.multiple_of(k, BLOCK), BLOCK)
                for jb in range(w // BLOCK):
                    m = dm_ref[k // BLOCK, (r * width + j * w) // BLOCK + jb]
                    if stage:
                        v = b_stage[cc, jnp.minimum(count, b_room - 1)]
                    else:
                        v = b_raw[cc, (j * 2 * blocks_k + i) * (w // BLOCK) + jb]
                    v = v.reshape(BLOCK // 16, 16, BLOCK)
                    cols = pl.ds(jb * BLOCK, BLOCK)
                    b_m[j, to, cols] = (v * mask_vector(m)[None]).reshape(BLOCK, BLOCK)
                    count = count + m
                return count

            seen[cc] = lax.fori_loop(0, 2 * blocks_k, body, seen[cc])

    kc = orbitals // 4

    far = jnp.where(hi < hi_n // 2, hi_n - 1, 0)
    near = jnp.where(hi < hi_n // 2, 0, 1)

    def o_copy(q, h, j, dest, sender):
        return pltpu.make_async_remote_copy(
            src_ref=res.at[q, j, pl.ds(pl.multiple_of(h * rows, rows), rows)],
            dst_ref=out_ref.at[:, pl.ds(pl.multiple_of(sender * width + j * w, BLOCK), w)],
            send_sem=o_send.at[q, h, j],
            recv_sem=o_recv.at[sender, j],
            device_id=(dest, c),
            device_id_type=MESH,
        )

    def o_local(h, j):
        return pltpu.make_async_copy(
            res.at[0, j, pl.ds(pl.multiple_of(h * rows, rows), rows)],
            out_ref.at[:, pl.ds(pl.multiple_of(r * width + j * w, BLOCK), w)],
            o_send.at[0, h, j],
        )

    def unit(q, j, start, count):
        g = (lo + q) % lo_n
        at = pl.ds(pl.multiple_of(start * rows, rows), count * rows)
        part = pl.ds(0, count * rows)
        acc[part] = jnp.zeros((count * rows, w), jnp.float32)

        def body(k, _):
            ks = pl.ds(pl.multiple_of(k * kc, kc), kc)
            acc[part] += jnp.dot(
                a_m[g, at, ks], b_m[j, ks, :], preferred_element_type=jnp.float32
            )
            return 0

        lax.fori_loop(0, orbitals // kc, body, 0)
        res[q, j, at] = acc[part].astype(jnp.bfloat16)
        for i in range(count):
            h = start + i
            dest = row_of(h, g)

            def wait_send(h=h, dest=dest):
                o_copy(q, h, j, dest, r).wait_send()

            def wait_local(h=h):
                o_local(h, j).wait()

            if q == 0:
                pl.when(hi != h)(lambda: o_copy(q, h, j, dest, r).start())
                pl.when(hi == h)(lambda: o_local(h, j).start())
                late.append((hi != h, wait_send))
                late.append((hi == h, wait_local))
            else:
                o_copy(q, h, j, dest, r).start()
                late.append((True, wait_send))

    def b_arrive(j):
        for e in range(1, x_n):
            for sign in (-1, 1):
                xx = x + sign * e
                there = jnp.logical_and(xx >= 0, xx < x_n)
                cc = xx * CORES + core
                pl.when(there)(lambda: b_wait(j, cc))
                onward = x - sign
                more = jnp.logical_and(there, jnp.logical_and(onward >= 0, onward < x_n))
                b_go(more, 0 if sign > 0 else 1, j, cc, onward * CORES + core)
                b_go(there, 2, j, cc, other)

    per_chunk = 2 * blocks_k * (w // BLOCK)
    needs = [-(-min(b_room, (j + 1) * per_chunk) // piece) for j in range(chunks)]

    def b_move(p, q):
        cc = (c + q) % n_col
        return pltpu.make_async_copy(
            b_raw.at[cc, b_part(p)], b_stage.at[cc, b_part(p)], staged.at[q])

    def b_finish(p):
        for xx in range(x_n):
            b_wait(p, xx * CORES + (core + 1) % CORES)
        if stage:
            for q in range(1, n_col):
                b_move(p, q).start()
            for q in range(1, n_col):
                b_move(p, q).wait()
            if p == 0:
                for own in own_b:
                    own.wait()
        else:
            own_b[p].wait()
        for j in range(chunks):
            if needs[j] == p + 1:
                mask_b(j)

    def line_arrive(d):
        for sign in (-1, 1):
            h = hi + sign * d
            there = jnp.logical_and(h >= 0, h < hi_n)
            pl.when(there)(lambda: a_wait(h, lo))
            onward = hi - sign
            more = jnp.logical_and(there, jnp.logical_and(onward >= 0, onward < hi_n))
            a_go(more, 0 if sign > 0 else 1, h, lo, row_of(onward, lo))
            a_lo_go(there, h)

    def at_distance(d):
        if d == 0:
            return [(hi, true)]
        out = []
        for sign in (-1, 1):
            h = hi + sign * d
            inside = jnp.logical_and(h >= 0, h < hi_n)
            out.append((h, jnp.logical_and(inside, h != far)))
        return out

    def lo_arrive(found):
        for h, there in found:
            for e in range(1, lo_n):
                for sign in (-1, 1):
                    l = lo + sign * e
                    ok = jnp.logical_and(there, jnp.logical_and(l >= 0, l < lo_n))
                    pl.when(ok)(lambda: a_wait(h, l))
                    onward = lo - sign
                    more = jnp.logical_and(ok, jnp.logical_and(onward >= 0, onward < lo_n))
                    a_go(more, 2 if sign > 0 else 3, h, l, row_of(hi, onward))
        for h, there in found:
            for q in range(1, lo_n):
                g = (lo + q) % lo_n
                pl.when(there)(lambda: mask_a(h, g))

    own_a.wait()
    mask_a(hi, lo)
    for d in range(1, hi_n):
        line_arrive(d)
        b_arrive(d - 1)
        for h, there in at_distance(d):
            pl.when(there)(lambda: mask_a(h, lo))
        lo_arrive(at_distance(d - 1))
        b_finish(d - 1)
    mask_a(far, lo)
    for p in range(hi_n - 1, chunks):
        b_arrive(p)
        b_finish(p)
    for j in range(chunks):
        unit(0, j, 0, hi_n)
    for j in range(chunks):
        for q in range(1, lo_n):
            unit(q, j, near, hi_n - 1)
    lo_arrive([(far, true)])
    for j in range(chunks):
        for q in range(1, lo_n):
            unit(q, j, far, 1)

    for q in range(1, n_row):
        sender = (r + q) % n_row
        for j in range(chunks):
            o_copy(0, 0, j, r, sender).wait_recv()
    for cond, wait in late:
        when_static(cond, wait)


def pack_kernel(dims, room, dense, t_ref, d_ref, tm_ref, dm_ref, pr_ref, pa_ref, pb_ref):
    n_row, n_col, _, _, _, chunks = dims
    a_room, b_room = room
    r = lax.axis_index("row")
    c = lax.axis_index("col")
    rows, orbitals = t_ref.shape
    _, piece_rows, width = d_ref.shape
    half, w = orbitals // 2, width // chunks
    blocks_k = piece_rows // BLOCK
    mask_row = (pr_ref[r * n_col + c] * rows) // BLOCK

    def a_body(jb, count):
        m = jnp.int32(1) if dense else tm_ref[mask_row, jb]

        @pl.when(jnp.logical_and(m > 0, count < a_room))
        def _():
            pa_ref[count] = t_ref[:, pl.ds(pl.multiple_of(jb * BLOCK, BLOCK), BLOCK)]

        return count + m

    a_count = lax.fori_loop(0, orbitals // BLOCK, a_body, jnp.int32(0))

    def a_clear(p, _):
        pa_ref[p] = jnp.zeros((rows, BLOCK), pa_ref.dtype)
        return 0

    lax.fori_loop(a_count, a_room, a_clear, 0)

    def b_body(i, count):
        kb, jh = i % blocks_k, i // blocks_k
        h, j = jh % 2, jh // 2
        k = h * half + c * piece_rows + kb * BLOCK
        for jb in range(w // BLOCK):
            m = jnp.int32(1) if dense else dm_ref[k // BLOCK, (r * width + j * w) // BLOCK + jb]

            @pl.when(jnp.logical_and(m > 0, count < b_room))
            def _():
                cols = pl.ds(pl.multiple_of(j * w + jb * BLOCK, BLOCK), BLOCK)
                pb_ref[count] = d_ref[h, pl.ds(pl.multiple_of(kb * BLOCK, BLOCK), BLOCK), cols]

            count = count + m
        return count

    b_count = lax.fori_loop(0, chunks * 2 * blocks_k, b_body, jnp.int32(0))

    def b_clear(p, _):
        pb_ref[p] = jnp.zeros((BLOCK, BLOCK), pb_ref.dtype)
        return 0

    lax.fori_loop(b_count, b_room, b_clear, 0)


def contract(dims, room, dense, number, tensor, density, tensor_mask, density_mask, pair_rows):
    n_row, n_col, hi_n, lo_n, x_n, chunks = dims
    a_room, b_room = room
    rows, orbitals = tensor.shape
    _, piece_rows, width = density.shape
    w = width // chunks
    bf16 = jnp.bfloat16
    any_spec = pl.BlockSpec(memory_space=pl.ANY)
    smem = pl.BlockSpec(memory_space=pltpu.SMEM)
    vmem = pl.BlockSpec(memory_space=pltpu.VMEM)
    packed = pl.pallas_call(
        functools.partial(pack_kernel, dims, room, dense),
        out_shape=[
            jax.ShapeDtypeStruct((a_room, rows, BLOCK), bf16),
            jax.ShapeDtypeStruct((b_room, BLOCK, BLOCK), bf16),
        ],
        in_specs=[vmem, vmem, smem, smem, smem],
        out_specs=[vmem, vmem],
        compiler_params=pltpu.CompilerParams(vmem_limit_bytes=60 << 20),
    )(tensor, density, tensor_mask, density_mask, pair_rows)
    return pl.pallas_call(
        functools.partial(kernel, dims, room),
        out_shape=jax.ShapeDtypeStruct((rows, orbitals), bf16),
        in_specs=[any_spec, any_spec, smem, smem, smem],
        out_specs=any_spec,
        scratch_shapes=[
            pltpu.VMEM((n_row, a_room, rows, BLOCK), bf16),
            pltpu.VMEM((lo_n, hi_n * rows, orbitals), bf16),
            pltpu.VMEM((n_col, b_room, BLOCK, BLOCK), bf16),
            pltpu.VMEM((chunks, orbitals, w), bf16),
            pltpu.VMEM((hi_n * rows, w), jnp.float32),
            pltpu.VMEM((lo_n, chunks, hi_n * rows, w), bf16),
            pltpu.SemaphoreType.DMA((n_row,)),
            pltpu.SemaphoreType.DMA((4, n_row)),
            pltpu.SemaphoreType.DMA((n_col, chunks)),
            pltpu.SemaphoreType.DMA((3, n_col, chunks)),
            pltpu.SemaphoreType.DMA((n_row, chunks)),
            pltpu.SemaphoreType.DMA((lo_n, hi_n, chunks)),
            pltpu.SemaphoreType.DMA((chunks + 1,)),
        ] + ([] if dense else [
            pltpu.VMEM((a_room, rows, BLOCK), bf16),
            pltpu.VMEM((n_col, b_room, BLOCK, BLOCK), bf16),
            pltpu.SemaphoreType.DMA((n_col + 1,)),
        ]),
        compiler_params=pltpu.CompilerParams(
            collective_id=number, has_side_effects=True, vmem_limit_bytes=60 << 20
        ),
    )(*packed, tensor_mask, density_mask, pair_rows)


def on_device(dims, *args):
    n_row, n_col, _, _, _, chunks = dims
    tensor, density, tensor_mask, density_mask, _ = args
    nb = tensor.shape[1] // BLOCK
    a_full = nb
    b_full = density.size // (BLOCK * BLOCK)

    def roomy(full, step, margin):
        wanted = full // 2 + margin * math.isqrt(full) // 2
        return min(full, -(-wanted // step) * step)

    small = (roomy(a_full, 1, 3), roomy(b_full, chunks, 4))
    a_most = jnp.max(jnp.sum(tensor_mask, axis=1))
    b_most = jnp.max(jnp.sum(
        density_mask.reshape(2, n_col, nb // 2 // n_col, n_row, nb // n_row), axis=(0, 2, 4)))
    fits = jnp.logical_and(a_most <= small[0], b_most <= small[1])
    return lax.cond(
        fits,
        functools.partial(contract, dims, small, False, 0),
        functools.partial(contract, dims, (a_full, b_full), True, 1),
        *args,
    )


def solution(mesh):
    n_row, n_col = mesh.shape["row"], mesh.shape["col"]
    hi_n = 1
    while hi_n * hi_n < n_row:
        hi_n *= 2
    dims = (n_row, n_col, hi_n, n_row // hi_n, n_col // CORES, max(4, hi_n))
    placed = (P(("row", "col"), None), P(None, "col", "row"), P(), P(), P())
    return jax.shard_map(
        functools.partial(on_device, dims),
        mesh=mesh,
        in_specs=placed,
        out_specs=P(("row", "col"), None),
        check_vma=False,
    )
```
